256 devices in a mesh: dp: 8 (over y, core), expert: 32 (over z, x).
Axes of the slice: x: 4, y: 4, z: 8, core: 2. Of those that a mesh axis runs over, the one named last changes fastest.
Arguments:
- tokens: bfloat16 [65536, 4096], P(('dp', 'expert')), may hold values from -6 to 6
- routes: int32 [65536, 2], P(('dp', 'expert')), may hold values from 0 to 31, all different within a row; in each aligned block of 256 rows (0 to 255, 256 to 511, ...) at most 32 rows name the same one
- route_weights: float32 [65536, 2], P(('dp', 'expert')), may hold values from 0.1 to 0.9
- placement: int32 [32], replicated, may hold values from 0 to 31, each once
- expert_weights: bfloat16 [32, 4096, 1024], P('expert', None, 'dp'), may hold values from -0.09375 to 0.09375
- grads: bfloat16 [32, 4096, 1024], P('expert', None, 'dp'), may hold values from -0.059814453 to 0.059814453
- first_moment: bfloat16 [32, 4096, 1024], P('expert', None, 'dp'), may hold values from -0.017944336 to 0.017944336
- second_moment: bfloat16 [32, 4096, 1024], P('expert', None, 'dp'), may hold values from 9.953976e-06 to 0.0009994507
Outputs:
- new_weights: bfloat16 [32, 4096, 1024], P('expert', None, 'dp')
- new_first: bfloat16 [32, 4096, 1024], P('expert', None, 'dp')
- new_second: bfloat16 [32, 4096, 1024], P('expert', None, 'dp')
- mixed: bfloat16 [65536, 1024], P(('dp', 'expert'))
The draws below stay inside these ranges and needn't reach their ends.
Inputs may be any that keep to these rules, and one draw needn't show every extreme that they name: `routes`: each token names two different experts; within the rows of one device no expert is named more than 32 times, a bound that some block reaches. `placement`: each expert appears exactly once.
All inputs are finite; a program needn't handle non-finite values.
Results may differ from the reference program's by a relative error of at most 0.0057.
Values may be sent and summed in bfloat16 or wider, within the bound.
A program may use at most 192 MiB of HBM per device.

```python
import math
import jax
import jax.numpy as jnp
import numpy as np
from jax import lax

D = 4096
HID = 1024
TOK_DEV = 256
EXPERTS = 32
CAP = 32
TOKENS = 65536
N_DP = 8
N_EXPERT = 32


def level_of(stream_key, shape, cuts, least, largest):
    level = 1.0
    for axis_at, parts in cuts:
        heights = jax.random.uniform(jax.random.fold_in(jax.random.fold_in(stream_key, 6), axis_at), (parts,), jnp.float32, least / len(cuts), largest / len(cuts))
        level = level * jnp.repeat(jnp.exp(heights), shape[axis_at] // parts).reshape((-1,) + (1,) * (len(shape) - 1 - axis_at))
    return level


def routed_block(own_key, own, number, rows, number_of, top, reach, lean):
    order = jax.random.permutation(own_key, number_of)
    crowded, common = shares(number_of, rows * top, reach, lean, True), shares(number_of, rows * top, reach, lean, False)
    places = jnp.arange(number_of)

    def named(lengths, turn):
        used = int((lengths > 0).sum())
        fixed = max(1, used // 4)
        passed = fixed + (places - fixed + turn * (used - fixed)) % max(1, number_of - fixed)
        return jnp.zeros((number_of,), jnp.int32).at[order[jnp.where(places < fixed, places, passed)]].set(jnp.asarray(lengths, jnp.int32))

    lengths = jnp.where(number % 4 == 0, named(crowded, number // 4), named(common, number - number // 4 - 1))
    mixed = jax.random.permutation(jax.random.fold_in(own, 3), number_of)
    donor, receiver = mixed[0:number_of // 2 * 2:2], mixed[1:number_of // 2 * 2:2]
    slack = jnp.minimum(lengths[donor] - 1, reach - lengths[receiver]) // 2
    slack = jnp.where((donor == order[0]) | (receiver == order[0]) | (lengths[receiver] == 0), 0, jnp.maximum(slack, 0))
    passed = jax.random.randint(jax.random.fold_in(own, 4), (number_of // 2,), 0, 1 << 20) % (slack + 1)
    lengths = lengths.at[donor].add(-passed).at[receiver].add(passed)
    members = jnp.searchsorted(jnp.cumsum(lengths), jnp.arange(rows * top), side="right").astype(jnp.int32)
    listing = members.reshape(top, rows).T
    listing = listing[jax.random.permutation(jax.random.fold_in(own, 1), rows)]
    turn = jax.random.randint(jax.random.fold_in(own, 2), (rows, 1), 0, top)
    return jnp.take_along_axis(listing, (jnp.arange(top)[None, :] + turn) % top, axis=1)


def shares(amount, total, bound, slope, full):
    portions = [(1 << 20) // math.isqrt(rank ** slope) + 1 for rank in range(1, amount + 1)]
    largest = bound if full else min(bound, max(-(-total // amount), total * portions[0] // sum(portions)))
    least = 1 if total - largest >= amount - 1 else 0
    counts, spare = [largest] + [least] * (amount - 1), total - largest - least * (amount - 1)
    while spare > 0:
        candidates = [i for i in range(1, amount) if counts[i] < largest] or [i for i in range(1, amount) if counts[i] < bound]
        pool, budget = sum([portions[i] for i in candidates]), spare
        for i in candidates:
            extra = min(bound - counts[i], max(1, budget * portions[i] // pool), spare)
            counts[i] = counts[i] + extra
            spare = spare - extra
    return np.array(counts)


def normal_values(key, shape, spread, most, cuts=(), held_as=jnp.bfloat16):
    values = spread * jax.random.normal(key, shape, jnp.float32)
    if cuts:
        values = values * level_of(key, shape, cuts, -0.22, 0.18)
    return jnp.clip(values, -most, most).astype(held_as)


def setup_inputs(seed: int = 0) -> dict:
    key_of = jax.random.split(jax.random.key(seed), 9)
    tokens = normal_values(key_of[0], (TOKENS, D), 1.0, 6.0, ((0, 256),))
    routes_keys = jax.random.split(jax.random.fold_in(key_of[1], 1), TOKENS // TOK_DEV)
    routes_turns = jax.random.permutation(jax.random.fold_in(key_of[1], 3), TOKENS // TOK_DEV)
    routes = jax.vmap(lambda own, number: routed_block(jax.random.fold_in(key_of[1], 2), own, number, TOK_DEV, EXPERTS, 2, CAP, 2))(routes_keys, routes_turns).reshape((TOKENS, 2))
    route_weights = jnp.clip(0.1 + 0.79999997 * jax.random.uniform(key_of[2], (TOKENS, 2), jnp.float32) ** level_of(key_of[2], (TOKENS, 2), ((0, 256),), -0.2, 0.2), 0.1, 0.9)
    placement = jax.random.permutation(key_of[3], EXPERTS).astype(jnp.int32)
    expert_weights = normal_values(key_of[4], (EXPERTS, D, HID), D ** -0.5, 0.09375, ((0, 32), (2, 8)))
    grads = normal_values(key_of[5], (EXPERTS, D, HID), 0.01, 0.059814453, ((0, 32), (2, 8)))
    first_moment = normal_values(key_of[6], (EXPERTS, D, HID), 0.003, 0.017944336, ((0, 32), (2, 8)))
    second_moment = jnp.clip(jnp.exp(math.log(0.0009994507) - 4.609234 * jax.random.uniform(key_of[7], (EXPERTS, D, HID), jnp.float32) ** level_of(key_of[7], (EXPERTS, D, HID), ((0, 32), (2, 8)), -0.2, 0.2)), 9.953975677490234e-06, 0.0009994507).astype(jnp.bfloat16)
    return dict(tokens=tokens, routes=routes, route_weights=route_weights, placement=placement, expert_weights=expert_weights, grads=grads, first_moment=first_moment, second_moment=second_moment)


beta_one = 0.9
beta_two = 0.999
learn_rate = 0.008
adam_eps = 1e-08

def adam_step(weight, gradient, first, second):
    grad_wide = gradient.astype(jnp.float32)
    first_wide = beta_one * first.astype(jnp.float32) + (1.0 - beta_one) * grad_wide
    second_wide = beta_two * second.astype(jnp.float32) + (1.0 - beta_two) * grad_wide * grad_wide
    updated = weight.astype(jnp.float32) - learn_rate * first_wide / (jnp.sqrt(second_wide) + adam_eps)
    return (updated.astype(jnp.bfloat16), first_wide.astype(jnp.bfloat16), second_wide.astype(jnp.bfloat16))

def reference(tokens, routes, route_weights, placement, expert_weights, grads, first_moment, second_moment):
    updated, first_low, second_low = adam_step(expert_weights, grads, first_moment, second_moment)
    new_weights = updated[placement]
    new_first = first_low[placement]
    new_second = second_low[placement]
    blocks = N_DP * N_EXPERT
    entries = routes.reshape(blocks, 2 * TOK_DEV).astype(jnp.int32)
    onehot = (entries[:, :, None] == jnp.arange(EXPERTS, dtype=jnp.int32)[None, None, :]).astype(jnp.int32)
    before = jnp.cumsum(onehot, axis=1) - onehot
    position = lax.optimization_barrier(jnp.sum(before * onehot, axis=2)).astype(jnp.int32)
    slot_index = (jnp.arange(blocks, dtype=jnp.int32)[:, None] * CAP + position).astype(jnp.int32)
    entry_ids = jnp.arange(blocks * 2 * TOK_DEV, dtype=jnp.int32).reshape(blocks, 2 * TOK_DEV)
    table = jnp.zeros((EXPERTS, blocks * CAP), jnp.int32).at[entries, slot_index].set(entry_ids // 2)

    def per_expert(expert_id):
        gathered = tokens[table[expert_id]]
        product = jnp.dot(gathered, updated[expert_id], preferred_element_type=jnp.float32)
        return jax.nn.silu(product).astype(jnp.bfloat16)
    acts = lax.map(per_expert, jnp.arange(EXPERTS, dtype=jnp.int32))
    picked = acts[entries, slot_index].reshape(TOKENS, 2, HID)
    mixed = lax.optimization_barrier(jnp.sum(route_weights[:, :, None] * picked.astype(jnp.float32), axis=1)).astype(jnp.bfloat16)
    return (new_weights, new_first, new_second, mixed)
```

```python
import jax
import jax.numpy as jnp
from jax import lax
from jax.sharding import Mesh, PartitionSpec as P

beta_one = 0.9
beta_two = 0.999
learn_rate = 0.008
adam_eps = 1e-08

Z_DIM = 8
X_DIM = 4


def adam_step(weight, gradient, first, second):
    grad_wide = gradient.astype(jnp.float32)
    first_wide = beta_one * first.astype(jnp.float32) + (1.0 - beta_one) * grad_wide
    second_wide = beta_two * second.astype(jnp.float32) + (1.0 - beta_two) * grad_wide * grad_wide
    updated = weight.astype(jnp.float32) - learn_rate * first_wide / (
        jnp.sqrt(second_wide) + adam_eps
    )
    return (
        updated.astype(jnp.bfloat16),
        first_wide.astype(jnp.bfloat16),
        second_wide.astype(jnp.bfloat16),
    )


def shards(
    tokens, routes, route_weights, placement, expert_weights, grads, first_moment, second_moment
):
    experts = Z_DIM * X_DIM
    width = tokens.shape[1]
    depth, piece = expert_weights.shape[1:]
    updated, first_low, second_low = adam_step(
        expert_weights[0], grads[0], first_moment[0], second_moment[0]
    )
    tok_count = tokens.shape[0]
    capacity = 4 * tok_count // experts
    expert_ids = jnp.arange(experts, dtype=jnp.int32)
    entries = routes.reshape(2 * tok_count)
    onehot = (entries[:, None] == expert_ids[None, :]).astype(jnp.int32)
    before = jnp.cumsum(onehot, axis=0) - onehot
    position = jnp.sum(before * onehot, axis=1)
    target_slot = entries * capacity + position
    select = (
        target_slot[:, None] == jnp.arange(experts * capacity, dtype=jnp.int32)[None, :]
    ).astype(jnp.bfloat16)
    select_pairs = select.reshape(tok_count, 2, experts * capacity)
    select_tokens = jnp.sum(select_pairs, axis=1)
    outgoing = jnp.einsum(
        "ts,td->sd", select_tokens, tokens, preferred_element_type=jnp.float32
    ).astype(jnp.bfloat16)
    received = lax.all_to_all(
        outgoing.reshape(experts, capacity, width), ("dp", "x"),
        split_axis=0, concat_axis=0, tiled=True,
    )
    slot_rows = received.reshape(experts * capacity, width)
    column = lax.all_gather(updated, "z", axis=0, tiled=False)
    served = lax.all_to_all(column, "dp", split_axis=0, concat_axis=0, tiled=True)
    full = served.transpose(1, 0, 2).reshape(depth, 8 * piece)
    state = jnp.stack(
        [a.reshape(experts, depth // experts, piece) for a in (updated, first_low, second_low)],
        axis=1,
    )
    spread = lax.all_to_all(state, ("z", "x"), split_axis=0, concat_axis=0, tiled=True)
    chosen = jnp.take(spread, placement, axis=0)
    collected = lax.all_to_all(chosen, ("z", "x"), split_axis=0, concat_axis=0, tiled=True)
    acts = jax.nn.silu(
        jnp.dot(slot_rows, full, preferred_element_type=jnp.float32)
    ).astype(jnp.bfloat16)
    hidden = acts.shape[1]
    returned = lax.all_to_all(
        acts.reshape(experts, capacity, hidden), ("dp", "x"), split_axis=0, concat_axis=0, tiled=True
    )
    back_rows = returned.reshape(experts * capacity, hidden)
    picked = jnp.einsum("tks,sh->tkh", select_pairs, back_rows, preferred_element_type=jnp.float32)
    mixed = jnp.sum(route_weights[:, :, None] * picked, axis=1).astype(jnp.bfloat16)
    return tuple(collected[:, i].reshape(1, depth, piece) for i in range(3)) + (mixed,)


def solution(mesh):
    grid = Mesh(mesh.devices.reshape(8, Z_DIM, X_DIM), ("dp", "z", "x"))
    rows = P(("dp", "z", "x"), None)
    state = P(("z", "x"), None, "dp")
    return jax.shard_map(
        shards,
        mesh=grid,
        in_specs=(rows, rows, rows, P(), state, state, state, state),
        out_specs=(state, state, state, rows),
        check_vma=False,
    )
```

```python
import jax
import jax.numpy as jnp
from jax import lax
from jax.experimental import pallas as pl
from jax.experimental.pallas import tpu as pltpu
from jax.sharding import PartitionSpec as P

beta_one = 0.9
beta_two = 0.999
learn_rate = 0.008
adam_eps = 1e-08

DP = 8
Z_DIM = 8
X_DIM = 4
EXPERTS = Z_DIM * X_DIM
MESH = pl.DeviceIdType.MESH


def kernel(
    placement_ref, routes_ref, routes_t_ref, weights_ref, tokens_ref, w_ref, g_ref, m_ref, v_ref,
    mixed_ref, final_ref,
    column, served, outgoing, slots, acts, back, spread, landed, chosen,
    ring_send, ring_recv, serve_send, serve_recv, serve_local,
    tok_send, tok_recv, ret_send, ret_recv, one_send, one_recv, two_send, two_recv, two_local,
):
    dp = lax.axis_index("dp")
    own = lax.axis_index("expert")
    z, x = own // X_DIM, own % X_DIM
    mine = dp * X_DIM + x
    cap = slots.shape[0] // EXPERTS
    block = spread.shape[1] // 3
    half = column.shape[1] // 2

    def plane_peer(p):
        return (p // X_DIM, z * X_DIM + p % X_DIM)

    def slot_rows(p):
        return pl.ds(pl.multiple_of(p * cap, cap), cap)

    barrier = pltpu.get_barrier_semaphore()

    @pl.loop(1, EXPERTS)
    def _(o):
        pl.semaphore_signal(
            barrier, inc=1, device_id=plane_peer((mine + o) % EXPERTS), device_id_type=MESH
        )
        pl.semaphore_signal(
            barrier, inc=1, device_id=(dp, (own + o) % EXPERTS), device_id_type=MESH
        )

    @pl.loop(0, EXPERTS)
    def _(j):
        rows = pl.ds(pl.multiple_of(j * block, block), block)
        grad = g_ref[rows, :].astype(jnp.float32)
        first = beta_one * m_ref[rows, :].astype(jnp.float32) + (1.0 - beta_one) * grad
        second = beta_two * v_ref[rows, :].astype(jnp.float32) + (1.0 - beta_two) * grad * grad
        updated = w_ref[rows, :].astype(jnp.float32) - learn_rate * first / (
            jnp.sqrt(second) + adam_eps
        )
        updated = updated.astype(jnp.bfloat16)
        column[z, rows, :] = updated
        spread[j, 0:block, :] = updated
        spread[j, block : 2 * block, :] = first.astype(jnp.bfloat16)
        spread[j, 2 * block : 3 * block, :] = second.astype(jnp.bfloat16)

    landed[own] = spread[own]
    pl.semaphore_wait(barrier, 2 * (EXPERTS - 1))

    def part(ref, at, h):
        return ref.at[at, pl.ds(h * half, half), :]

    def ring_copy(way, step, h, source):
        to = (z + (1 if way == 0 else Z_DIM - 1)) % Z_DIM
        return pltpu.make_async_remote_copy(
            src_ref=part(column, source, h),
            dst_ref=part(column, source, h),
            send_sem=ring_send.at[way, step, h],
            recv_sem=ring_recv.at[way, step, h],
            device_id=(dp, to * X_DIM + x),
            device_id_type=MESH,
        )

    def ring_steps(way, step):
        if step < 3:
            return (0, 1)
        return (way,)

    def ring_source(way, step):
        return (z + (Z_DIM - step if way == 0 else step)) % Z_DIM

    def serve_copy(source, h, sender, target):
        return pltpu.make_async_remote_copy(
            src_ref=part(column, source, h),
            dst_ref=part(served, sender, h),
            send_sem=serve_send.at[source, h],
            recv_sem=serve_recv.at[sender, h],
            device_id=(target, own),
            device_id_type=MESH,
        )

    def serve_own(h):
        return pltpu.make_async_copy(part(column, dp, h), part(served, dp, h), serve_local.at[h])

    def serve(source, h):
        @pl.when(source != dp)
        def _():
            serve_copy(source, h, dp, source).start()

        @pl.when(source == dp)
        def _():
            serve_own(h).start()

    def ring_hop(step):
        for h in (0, 1):
            for way in (0, 1):
                if h not in ring_steps(way, step):
                    continue
                source = ring_source(way, step + 1)
                ring_copy(way, step, h, source).wait_recv()
                if step < 3 and h in ring_steps(way, step + 1):
                    ring_copy(way, step + 1, h, source).start()
                serve(source, h)

    for h in (0, 1):
        for way in (0, 1):
            ring_copy(way, 0, h, z).start()
    for h in (0, 1):
        serve(z, h)

    tok_count = tokens_ref.shape[0]

    def tok_copy(p, sender):
        return pltpu.make_async_remote_copy(
            src_ref=outgoing.at[slot_rows(p), :],
            dst_ref=slots.at[slot_rows(sender), :],
            send_sem=tok_send.at[p],
            recv_sem=tok_recv.at[sender],
            device_id=plane_peer(p),
            device_id_type=MESH,
        )

    named = routes_t_ref[...]
    ids = lax.broadcasted_iota(jnp.int32, (EXPERTS, tok_count), 0)
    hits = [ids == named[k : k + 1, :] for k in (0, 1)]
    both = jnp.where(hits[0] | hits[1], 1.0, 0.0).astype(jnp.bfloat16)
    row = lax.broadcasted_iota(jnp.int32, (tok_count, tok_count), 0)
    col = lax.broadcasted_iota(jnp.int32, (tok_count, tok_count), 1)
    earlier = jnp.where(row < col, 1.0, 0.0).astype(jnp.bfloat16)
    before = jnp.dot(both, earlier, preferred_element_type=jnp.float32)
    wide = [
        named[k : k + 1, :].astype(jnp.float32) * cap
        + jnp.sum(jnp.where(hits[k], before, 0.0), axis=0, keepdims=True)
        for k in (0, 1)
    ]
    group = 8 * cap
    width = tokens_ref.shape[1]
    chunk = 1024

    @pl.loop(0, 4)
    def _(q):
        first_row = ((dp // 2 + q) % 4) * group
        slot_id = (first_row + lax.broadcasted_iota(jnp.int32, (group, tok_count), 0)).astype(
            jnp.float32
        )
        pick = jnp.where((slot_id == wide[0]) | (slot_id == wide[1]), 1.0, 0.0).astype(jnp.bfloat16)
        for c in range(width // chunk):
            outgoing[pl.ds(pl.multiple_of(first_row, group), group), c * chunk : (c + 1) * chunk] = (
                jnp.dot(
                    pick,
                    tokens_ref[:, c * chunk : (c + 1) * chunk],
                    preferred_element_type=jnp.float32,
                ).astype(jnp.bfloat16)
            )

        @pl.loop(0, 8)
        def _(i):
            p = ((dp // 2 + q) % 4) * 8 + (mine + i) % 8

            @pl.when(p != mine)
            def _():
                tok_copy(p, mine).start()

            @pl.when(p == mine)
            def _():
                slots[slot_rows(mine), :] = outgoing[slot_rows(mine), :]

    def one_copy(j, sender):
        return pltpu.make_async_remote_copy(
            src_ref=spread.at[j],
            dst_ref=landed.at[sender],
            send_sem=one_send.at[j],
            recv_sem=one_recv.at[sender],
            device_id=(dp, j),
            device_id_type=MESH,
        )

    def two_copy(j, sender):
        return pltpu.make_async_remote_copy(
            src_ref=chosen.at[j],
            dst_ref=final_ref.at[sender],
            send_sem=two_send.at[j],
            recv_sem=two_recv.at[sender],
            device_id=(dp, j),
            device_id_type=MESH,
        )

    two_own = pltpu.make_async_copy(chosen.at[own], final_ref.at[own], two_local)

    ring_hop(0)
    ring_hop(1)

    @pl.loop(1, EXPERTS)
    def _(o):
        one_copy((own + o) % EXPERTS, own).start()

    ring_hop(2)
    ring_hop(3)

    @pl.loop(0, DP)
    def _(s):
        @pl.when(s != dp)
        def _():
            for h in (0, 1):
                serve_copy(dp, h, s, s).wait_recv()

        @pl.when(s == dp)
        def _():
            for h in (0, 1):
                serve_own(h).wait()

    def ret_copy(p, sender):
        return pltpu.make_async_remote_copy(
            src_ref=acts.at[slot_rows(p), :],
            dst_ref=back.at[slot_rows(sender), :],
            send_sem=ret_send.at[p],
            recv_sem=ret_recv.at[sender],
            device_id=plane_peer(p),
            device_id_type=MESH,
        )

    @pl.loop(0, 4)
    def _(q):
        base = ((dp // 2 + q) % 4) * 8
        rows = pl.ds(pl.multiple_of(base * cap, group), group)

        @pl.loop(0, 8)
        def _(i):
            p = base + i

            @pl.when(p != mine)
            def _():
                tok_copy(p, p).wait_recv()

        @pl.loop(0, DP // 2)
        def _(n):
            right = jnp.concatenate([served[2 * n], served[2 * n + 1]], axis=1)
            total = jnp.dot(slots[rows, :], right, preferred_element_type=jnp.float32)
            acts[rows, pl.ds(pl.multiple_of(n * 256, 256), 256)] = (
                total / (1.0 + jnp.exp(-total))
            ).astype(jnp.bfloat16)

        @pl.loop(0, 8)
        def _(i):
            p = base + (mine + i) % 8

            @pl.when(p != mine)
            def _():
                ret_copy(p, mine).start()

            @pl.when(p == mine)
            def _():
                back[slot_rows(mine), :] = acts[slot_rows(mine), :]

    @pl.loop(1, EXPERTS)
    def _(o):
        p = (own + EXPERTS - o) % EXPERTS
        one_copy(p, p).wait_recv()

    @pl.loop(0, EXPERTS)
    def _(j):
        chosen[j] = landed[placement_ref[j]]

    @pl.loop(1, EXPERTS)
    def _(o):
        two_copy((own + o) % EXPERTS, own).start()

    two_own.start()

    tall_named = routes_ref[...]
    lanes = lax.broadcasted_iota(jnp.int32, (tok_count, EXPERTS), 1)
    tall_hits = [lanes == tall_named[:, k : k + 1] for k in (0, 1)]
    tall_both = jnp.where(tall_hits[0] | tall_hits[1], 1.0, 0.0).astype(jnp.bfloat16)
    later = jnp.where(col < row, 1.0, 0.0).astype(jnp.bfloat16)
    tall_before = jnp.dot(later, tall_both, preferred_element_type=jnp.float32)
    slot_lane = lax.broadcasted_iota(jnp.int32, (tok_count, EXPERTS * cap), 1).astype(jnp.float32)
    tall_pick = []
    for k in (0, 1):
        slot = tall_named[:, k : k + 1].astype(jnp.float32) * cap + jnp.sum(
            jnp.where(tall_hits[k], tall_before, 0.0), axis=1, keepdims=True
        )
        tall_pick.append(jnp.where(slot_lane == slot, 1.0, 0.0).astype(jnp.bfloat16))

    @pl.loop(1, EXPERTS)
    def _(o):
        p = (mine + EXPERTS - o) % EXPERTS
        ret_copy(p, p).wait_recv()

    gain = weights_ref[...]
    for c in range(2):
        cols = slice(c * 512, (c + 1) * 512)
        got = [
            jnp.dot(tall_pick[k], back[:, cols], preferred_element_type=jnp.float32) for k in (0, 1)
        ]
        mixed_ref[:, cols] = (gain[:, 0:1] * got[0] + gain[:, 1:2] * got[1]).astype(jnp.bfloat16)

    @pl.loop(1, EXPERTS)
    def _(o):
        p = (mine + o) % EXPERTS
        tok_copy(p, mine).wait_send()
        ret_copy(p, mine).wait_send()
        j = (own + o) % EXPERTS
        one_copy(j, own).wait_send()
        two_copy(j, own).wait_send()

    for step in range(4):
        for way in (0, 1):
            for h in ring_steps(way, step):
                ring_copy(way, step, h, ring_source(way, step)).wait_send()

    @pl.loop(0, Z_DIM)
    def _(s):
        @pl.when(s != dp)
        def _():
            for h in (0, 1):
                serve_copy(s, h, dp, s).wait_send()

    @pl.loop(1, EXPERTS)
    def _(o):
        p = (own + EXPERTS - o) % EXPERTS
        two_copy(p, p).wait_recv()

    two_own.wait()


def shards(
    tokens, routes, route_weights, placement, expert_weights, grads, first_moment, second_moment
):
    depth, piece = expert_weights.shape[1:]
    count, width = tokens.shape
    hidden = DP * piece
    cap = 4 * count // EXPERTS
    block = depth // EXPERTS
    vmem = pl.BlockSpec(memory_space=pltpu.VMEM)
    dma = pltpu.SemaphoreType.DMA
    mixed, final = pl.pallas_call(
        kernel,
        out_shape=(
            jax.ShapeDtypeStruct((count, hidden), jnp.bfloat16),
            jax.ShapeDtypeStruct((EXPERTS, 3 * block, piece), jnp.bfloat16),
        ),
        in_specs=[pl.BlockSpec(memory_space=pltpu.SMEM)] + [vmem] * 8,
        out_specs=(vmem, pl.BlockSpec(memory_space=pl.ANY)),
        scratch_shapes=[
            pltpu.VMEM((Z_DIM, depth, piece), jnp.bfloat16),
            pltpu.VMEM((DP, depth, piece), jnp.bfloat16),
            pltpu.VMEM((EXPERTS * cap, width), jnp.bfloat16),
            pltpu.VMEM((EXPERTS * cap, width), jnp.bfloat16),
            pltpu.VMEM((EXPERTS * cap, hidden), jnp.bfloat16),
            pltpu.VMEM((EXPERTS * cap, hidden), jnp.bfloat16),
            pltpu.VMEM((EXPERTS, 3 * block, piece), jnp.bfloat16),
            pltpu.VMEM((EXPERTS, 3 * block, piece), jnp.bfloat16),
            pltpu.VMEM((EXPERTS, 3 * block, piece), jnp.bfloat16),
            dma((2, 4, 2)),
            dma((2, 4, 2)),
            dma((Z_DIM, 2)),
            dma((DP, 2)),
            dma((2,)),
        ]
        + [dma((EXPERTS,))] * 8
        + [dma],
        compiler_params=pltpu.CompilerParams(
            collective_id=0, has_side_effects=True, vmem_limit_bytes=60 * 1024 * 1024
        ),
    )(
        placement, routes, routes.T, route_weights, tokens,
        expert_weights[0], grads[0], first_moment[0], second_moment[0],
    )
    state = final.reshape(EXPERTS, 3, block, piece)
    return tuple(state[:, i].reshape(1, depth, piece) for i in range(3)) + (mixed,)


def solution(mesh):
    rows = P(("dp", "expert"), None)
    state = P("expert", None, "dp")
    return jax.shard_map(
        shards,
        mesh=mesh,
        in_specs=(rows, rows, rows, P(), state, state, state, state),
        out_specs=(state, state, state, rows),
        check_vma=False,
    )
```

```python
import jax
import jax.numpy as jnp
from jax import lax
from jax.experimental import pallas as pl
from jax.experimental.pallas import tpu as pltpu
from jax.sharding import PartitionSpec as P

beta_one = 0.9
beta_two = 0.999
learn_rate = 0.008
adam_eps = 1e-08

DP = 8
Z_DIM = 8
X_DIM = 4
EXPERTS = Z_DIM * X_DIM
WAVES = 8
MESH = pl.DeviceIdType.MESH


def kernel(
    placement_ref, routes_ref, routes_t_ref, weights_ref, tokens_ref, w_ref, g_ref, m_ref, v_ref,
    mixed_ref, final_ref,
    column, served, outgoing, slots, acts, back, spread, landed, chosen,
    ring_send, ring_recv, serve_send, serve_recv, serve_local,
    tok_send, tok_recv, ret_send, ret_recv, one_send, one_recv, two_send, two_recv, two_local,
):
    dp = lax.axis_index("dp")
    own = lax.axis_index("expert")
    z, x = own // X_DIM, own % X_DIM
    mine = dp * X_DIM + x
    cap = slots.shape[0] // EXPERTS
    block = spread.shape[1] // 3
    part_rows = column.shape[1] // WAVES

    def plane_peer(p):
        return (p // X_DIM, z * X_DIM + p % X_DIM)

    def slot_rows(p):
        return pl.ds(pl.multiple_of(p * cap, cap), cap)

    barrier = pltpu.get_barrier_semaphore()

    @pl.loop(1, EXPERTS)
    def _(o):
        pl.semaphore_signal(
            barrier, inc=1, device_id=plane_peer((mine + o) % EXPERTS), device_id_type=MESH
        )
        pl.semaphore_signal(
            barrier, inc=1, device_id=(dp, (own + o) % EXPERTS), device_id_type=MESH
        )

    @pl.loop(0, EXPERTS)
    def _(j):
        rows = pl.ds(pl.multiple_of(j * block, block), block)
        grad = g_ref[rows, :].astype(jnp.float32)
        first = beta_one * m_ref[rows, :].astype(jnp.float32) + (1.0 - beta_one) * grad
        second = beta_two * v_ref[rows, :].astype(jnp.float32) + (1.0 - beta_two) * grad * grad
        updated = w_ref[rows, :].astype(jnp.float32) - learn_rate * first / (
            jnp.sqrt(second) + adam_eps
        )
        updated = updated.astype(jnp.bfloat16)
        column[z, rows, :] = updated
        spread[j, 0:block, :] = updated
        spread[j, block : 2 * block, :] = first.astype(jnp.bfloat16)
        spread[j, 2 * block : 3 * block, :] = second.astype(jnp.bfloat16)

    landed[own] = spread[own]
    pl.semaphore_wait(barrier, 2 * (EXPERTS - 1))

    def part(ref, at, h):
        return ref.at[at, pl.ds(pl.multiple_of(h * part_rows, part_rows), part_rows), :]

    def ring_copy(way, step, h, source):
        to = (z + (1 if way == 0 else Z_DIM - 1)) % Z_DIM
        return pltpu.make_async_remote_copy(
            src_ref=part(column, source, h),
            dst_ref=part(column, source, h),
            send_sem=ring_send.at[way, step, h],
            recv_sem=ring_recv.at[way, step, h],
            device_id=(dp, to * X_DIM + x),
            device_id_type=MESH,
        )

    def ring_source(way, step):
        return (z + (Z_DIM - step if way == 0 else step)) % Z_DIM

    def serve_copy(source, h, sender, target):
        return pltpu.make_async_remote_copy(
            src_ref=part(column, source, h),
            dst_ref=part(served, sender, h),
            send_sem=serve_send.at[source, h],
            recv_sem=serve_recv.at[sender, h],
            device_id=(target, own),
            device_id_type=MESH,
        )

    def serve_own(h):
        return pltpu.make_async_copy(part(column, dp, h), part(served, dp, h), serve_local.at[h])

    def serve(source, h):
        @pl.when(source != dp)
        def _():
            serve_copy(source, h, dp, source).start()

        @pl.when(source == dp)
        def _():
            serve_own(h).start()

    def ring_start(h):
        for way in (0, 1):
            ring_copy(way, 0, h, z).start()
        serve(z, h)

    def ring_hop(step, h, parity):
        for way in (0, 1):
            if step == 3 and way != parity:
                continue
            source = ring_source(way, step + 1)
            ring_copy(way, step, h, source).wait_recv()
            if step < 2 or (step == 2 and way == parity):
                ring_copy(way, step + 1, h, source).start()
            serve(source, h)

    def ring_waves(first, last):
        @pl.loop(first, last)
        def _(v):
            for step in range(3):
                for parity in (0, 1):
                    ring_hop(step, 2 * v + parity, parity)

            @pl.when(v < WAVES // 2 - 1)
            def _():
                for parity in (0, 1):
                    ring_start(2 * v + 2 + parity)

            for parity in (0, 1):
                ring_hop(3, 2 * v + parity, parity)

    for parity in (0, 1):
        ring_start(parity)

    tok_count = tokens_ref.shape[0]

    def tok_copy(p, sender):
        return pltpu.make_async_remote_copy(
            src_ref=outgoing.at[slot_rows(p), :],
            dst_ref=slots.at[slot_rows(sender), :],
            send_sem=tok_send.at[p],
            recv_sem=tok_recv.at[sender],
            device_id=plane_peer(p),
            device_id_type=MESH,
        )

    named = routes_t_ref[...]
    ids = lax.broadcasted_iota(jnp.int32, (EXPERTS, tok_count), 0)
    hits = [ids == named[k : k + 1, :] for k in (0, 1)]
    both = jnp.where(hits[0] | hits[1], 1.0, 0.0).astype(jnp.bfloat16)
    row = lax.broadcasted_iota(jnp.int32, (tok_count, tok_count), 0)
    col = lax.broadcasted_iota(jnp.int32, (tok_count, tok_count), 1)
    earlier = jnp.where(row < col, 1.0, 0.0).astype(jnp.bfloat16)
    before = jnp.dot(both, earlier, preferred_element_type=jnp.float32)
    wide = [
        named[k : k + 1, :].astype(jnp.float32) * cap
        + jnp.sum(jnp.where(hits[k], before, 0.0), axis=0, keepdims=True)
        for k in (0, 1)
    ]
    group = 8 * cap
    width = tokens_ref.shape[1]
    chunk = 1024

    @pl.loop(0, 4)
    def _(q):
        first_row = ((dp // 2 + q) % 4) * group
        slot_id = (first_row + lax.broadcasted_iota(jnp.int32, (group, tok_count), 0)).astype(
            jnp.float32
        )
        pick = jnp.where((slot_id == wide[0]) | (slot_id == wide[1]), 1.0, 0.0).astype(jnp.bfloat16)
        for c in range(width // chunk):
            outgoing[pl.ds(pl.multiple_of(first_row, group), group), c * chunk : (c + 1) * chunk] = (
                jnp.dot(
                    pick,
                    tokens_ref[:, c * chunk : (c + 1) * chunk],
                    preferred_element_type=jnp.float32,
                ).astype(jnp.bfloat16)
            )

        @pl.loop(0, 8)
        def _(i):
            p = ((dp // 2 + q) % 4) * 8 + (mine + i) % 8

            @pl.when(p != mine)
            def _():
                tok_copy(p, mine).start()

            @pl.when(p == mine)
            def _():
                slots[slot_rows(mine), :] = outgoing[slot_rows(mine), :]

    def one_copy(j, sender):
        return pltpu.make_async_remote_copy(
            src_ref=spread.at[j],
            dst_ref=landed.at[sender],
            send_sem=one_send.at[j],
            recv_sem=one_recv.at[sender],
            device_id=(dp, j),
            device_id_type=MESH,
        )

    def two_copy(j, sender):
        return pltpu.make_async_remote_copy(
            src_ref=chosen.at[j],
            dst_ref=final_ref.at[sender],
            send_sem=two_send.at[j],
            recv_sem=two_recv.at[sender],
            device_id=(dp, j),
            device_id_type=MESH,
        )

    two_own = pltpu.make_async_copy(chosen.at[own], final_ref.at[own], two_local)

    ring_waves(0, WAVES // 4)

    @pl.loop(1, EXPERTS)
    def _(o):
        one_copy((own + o) % EXPERTS, own).start()

    ring_waves(WAVES // 4, WAVES // 2)

    @pl.loop(1, EXPERTS)
    def _(o):
        p = (own + EXPERTS - o) % EXPERTS
        one_copy(p, p).wait_recv()

    @pl.loop(0, EXPERTS)
    def _(j):
        chosen[j] = landed[placement_ref[j]]

    @pl.loop(1, EXPERTS)
    def _(o):
        two_copy((own + o) % EXPERTS, own).start()

    two_own.start()

    @pl.loop(0, DP)
    def _(s):
        @pl.when(s != dp)
        def _():
            @pl.loop(0, WAVES)
            def _(h):
                serve_copy(dp, h, s, s).wait_recv()

        @pl.when(s == dp)
        def _():
            @pl.loop(0, WAVES)
            def _(h):
                serve_own(h).wait()

    def ret_copy(p, sender):
        return pltpu.make_async_remote_copy(
            src_ref=acts.at[slot_rows(p), :],
            dst_ref=back.at[slot_rows(sender), :],
            send_sem=ret_send.at[p],
            recv_sem=ret_recv.at[sender],
            device_id=plane_peer(p),
            device_id_type=MESH,
        )

    @pl.loop(0, 4)
    def _(q):
        base = ((dp // 2 + q) % 4) * 8
        rows = pl.ds(pl.multiple_of(base * cap, group), group)

        @pl.loop(0, 8)
        def _(i):
            p = base + i

            @pl.when(p != mine)
            def _():
                tok_copy(p, p).wait_recv()

        @pl.loop(0, DP // 2)
        def _(n):
            right = jnp.concatenate([served[2 * n], served[2 * n + 1]], axis=1)
            total = jnp.dot(slots[rows, :], right, preferred_element_type=jnp.float32)
            acts[rows, pl.ds(pl.multiple_of(n * 256, 256), 256)] = (
                total / (1.0 + jnp.exp(-total))
            ).astype(jnp.bfloat16)

        @pl.loop(0, 8)
        def _(i):
            p = base + (mine + i) % 8

            @pl.when(p != mine)
            def _():
                ret_copy(p, mine).start()

            @pl.when(p == mine)
            def _():
                back[slot_rows(mine), :] = acts[slot_rows(mine), :]

    tall_named = routes_ref[...]
    lanes = lax.broadcasted_iota(jnp.int32, (tok_count, EXPERTS), 1)
    tall_hits = [lanes == tall_named[:, k : k + 1] for k in (0, 1)]
    tall_both = jnp.where(tall_hits[0] | tall_hits[1], 1.0, 0.0).astype(jnp.bfloat16)
    later = jnp.where(col < row, 1.0, 0.0).astype(jnp.bfloat16)
    tall_before = jnp.dot(later, tall_both, preferred_element_type=jnp.float32)
    slot_lane = lax.broadcasted_iota(jnp.int32, (tok_count, EXPERTS * cap), 1).astype(jnp.float32)
    tall_pick = []
    for k in (0, 1):
        slot = tall_named[:, k : k + 1].astype(jnp.float32) * cap + jnp.sum(
            jnp.where(tall_hits[k], tall_before, 0.0), axis=1, keepdims=True
        )
        tall_pick.append(jnp.where(slot_lane == slot, 1.0, 0.0).astype(jnp.bfloat16))

    @pl.loop(1, EXPERTS)
    def _(o):
        p = (mine + EXPERTS - o) % EXPERTS
        ret_copy(p, p).wait_recv()

    gain = weights_ref[...]
    for c in range(2):
        cols = slice(c * 512, (c + 1) * 512)
        got = [
            jnp.dot(tall_pick[k], back[:, cols], preferred_element_type=jnp.float32) for k in (0, 1)
        ]
        mixed_ref[:, cols] = (gain[:, 0:1] * got[0] + gain[:, 1:2] * got[1]).astype(jnp.bfloat16)

    @pl.loop(1, EXPERTS)
    def _(o):
        p = (mine + o) % EXPERTS
        tok_copy(p, mine).wait_send()
        ret_copy(p, mine).wait_send()
        j = (own + o) % EXPERTS
        one_copy(j, own).wait_send()
        two_copy(j, own).wait_send()

    @pl.loop(0, WAVES // 2)
    def _(v):
        for parity in (0, 1):
            for step in range(4):
                for way in (0, 1):
                    if step < 3 or way == parity:
                        ring_copy(way, step, 2 * v + parity, ring_source(way, step)).wait_send()

    @pl.loop(0, Z_DIM)
    def _(s):
        @pl.when(s != dp)
        def _():
            @pl.loop(0, WAVES)
            def _(h):
                serve_copy(s, h, dp, s).wait_send()

    @pl.loop(1, EXPERTS)
    def _(o):
        p = (own + EXPERTS - o) % EXPERTS
        two_copy(p, p).wait_recv()

    two_own.wait()


def shards(
    tokens, routes, route_weights, placement, expert_weights, grads, first_moment, second_moment
):
    depth, piece = expert_weights.shape[1:]
    count, width = tokens.shape
    hidden = DP * piece
    cap = 4 * count // EXPERTS
    block = depth // EXPERTS
    vmem = pl.BlockSpec(memory_space=pltpu.VMEM)
    dma = pltpu.SemaphoreType.DMA
    mixed, final = pl.pallas_call(
        kernel,
        out_shape=(
            jax.ShapeDtypeStruct((count, hidden), jnp.bfloat16),
            jax.ShapeDtypeStruct((EXPERTS, 3 * block, piece), jnp.bfloat16),
        ),
        in_specs=[pl.BlockSpec(memory_space=pltpu.SMEM)] + [vmem] * 8,
        out_specs=(vmem, pl.BlockSpec(memory_space=pl.ANY)),
        scratch_shapes=[
            pltpu.VMEM((Z_DIM, depth, piece), jnp.bfloat16),
            pltpu.VMEM((DP, depth, piece), jnp.bfloat16),
            pltpu.VMEM((EXPERTS * cap, width), jnp.bfloat16),
            pltpu.VMEM((EXPERTS * cap, width), jnp.bfloat16),
            pltpu.VMEM((EXPERTS * cap, hidden), jnp.bfloat16),
            pltpu.VMEM((EXPERTS * cap, hidden), jnp.bfloat16),
            pltpu.VMEM((EXPERTS, 3 * block, piece), jnp.bfloat16),
            pltpu.VMEM((EXPERTS, 3 * block, piece), jnp.bfloat16),
            pltpu.VMEM((EXPERTS, 3 * block, piece), jnp.bfloat16),
            dma((2, 4, WAVES)),
            dma((2, 4, WAVES)),
            dma((Z_DIM, WAVES)),
            dma((DP, WAVES)),
            dma((WAVES,)),
        ]
        + [dma((EXPERTS,))] * 8
        + [dma],
        compiler_params=pltpu.CompilerParams(
            collective_id=0, has_side_effects=True, vmem_limit_bytes=60 * 1024 * 1024
        ),
    )(
        placement, routes, routes.T, route_weights, tokens,
        expert_weights[0], grads[0], first_moment[0], second_moment[0],
    )
    state = final.reshape(EXPERTS, 3, block, piece)
    return tuple(state[:, i].reshape(1, depth, piece) for i in range(3)) + (mixed,)


def solution(mesh):
    rows = P(("dp", "expert"), None)
    state = P("expert", None, "dp")
    return jax.shard_map(
        shards,
        mesh=mesh,
        in_specs=(rows, rows, rows, P(), state, state, state, state),
        out_specs=(state, state, state, rows),
        check_vma=False,
    )
```

```python
import jax
import jax.numpy as jnp
from jax import lax
from jax.experimental import pallas as pl
from jax.experimental.pallas import tpu as pltpu
from jax.sharding import PartitionSpec as P

beta_one = 0.9
beta_two = 0.999
learn_rate = 0.008
adam_eps = 1e-08

DP = 8
Z_DIM = 8
X_DIM = 4
EXPERTS = Z_DIM * X_DIM
WAVES = 4
LATE = 1
MESH = pl.DeviceIdType.MESH


def kernel(
    placement_ref, named_ref, gains_ref, tokens_in, w_in, g_in, m_in, v_in,
    mixed_ref, final_ref,
    tokens_ref, w_ref, g_ref, m_ref, v_ref, total,
    column, served, outgoing, slots, acts, back, spread, landed, chosen,
    ring_send, ring_recv, serve_send, serve_recv, serve_local,
    tok_send, tok_recv, ret_send, ret_recv, one_send, one_recv, two_send, two_recv, two_local, load,
):
    dp = lax.axis_index("dp")
    own = lax.axis_index("expert")
    z, x = own // X_DIM, own % X_DIM
    mine = dp * X_DIM + x
    cap = slots.shape[0] // EXPERTS
    block = spread.shape[1] // 3
    part_rows = column.shape[1] // WAVES

    def plane_peer(p):
        return (p // X_DIM, z * X_DIM + p % X_DIM)

    def slot_rows(p):
        return pl.ds(pl.multiple_of(p * cap, cap), cap)

    loads = [
        pltpu.make_async_copy(source, target, load.at[i])
        for i, (source, target) in enumerate(
            (
                (w_in, w_ref), (g_in, g_ref), (m_in, m_ref), (v_in, v_ref), (tokens_in, tokens_ref)
            )
        )
    ]
    for copy in loads:
        copy.start()

    def place(n):
        y_step, x_step = n % 4, (n // 4 + n) % 4
        chip_y, core = (dp // 2 + y_step) % 4, (dp + n // 16) % 2
        return (chip_y * 2 + core) * X_DIM + (x + x_step) % X_DIM

    def mirror(n):
        y_step, x_step = (4 - n % 4) % 4, (8 - (n // 4) % 4 - n % 4) % 4
        return (n // 16) * 16 + ((x_step + 4 - y_step) % 4) * 4 + y_step

    def slot_ids(row):
        n = row >> 5
        y_step, x_step = n & 3, ((n >> 2) + n) & 3
        chip_y, core = (dp // 2 + y_step) & 3, (dp + (n >> 4)) & 1
        served_by = (chip_y * 2 + core) * X_DIM + ((x + x_step) & 3)
        return (served_by * cap + (row & (cap - 1))).astype(jnp.float32)

    def owner(n):
        k = n % Z_DIM
        z_step = (k % 2) * ((k + 1) // 2) + (1 - k % 2) * (Z_DIM - k // 2)
        return ((z + z_step) % Z_DIM) * X_DIM + (x + n // Z_DIM + n) % X_DIM

    barrier = pltpu.get_barrier_semaphore()

    @pl.loop(1, EXPERTS)
    def _(o):
        pl.semaphore_signal(
            barrier, inc=1, device_id=plane_peer((mine + o) % EXPERTS), device_id_type=MESH
        )
        pl.semaphore_signal(
            barrier, inc=1, device_id=(dp, (own + o) % EXPERTS), device_id_type=MESH
        )

    for copy in loads[:4]:
        copy.wait()

    @pl.loop(0, EXPERTS)
    def _(j):
        rows = pl.ds(pl.multiple_of(j * block, block), block)
        grad = g_ref[rows, :].astype(jnp.float32)
        first = beta_one * m_ref[rows, :].astype(jnp.float32) + (1.0 - beta_one) * grad
        second = beta_two * v_ref[rows, :].astype(jnp.float32) + (1.0 - beta_two) * grad * grad
        updated = w_ref[rows, :].astype(jnp.float32) - learn_rate * first / (
            jnp.sqrt(second) + adam_eps
        )
        updated = updated.astype(jnp.bfloat16)
        column[z, rows, :] = updated
        spread[j, 0:block, :] = updated
        spread[j, block : 2 * block, :] = first.astype(jnp.bfloat16)
        spread[j, 2 * block : 3 * block, :] = second.astype(jnp.bfloat16)

    landed[own] = spread[own]
    pl.semaphore_wait(barrier, 2 * (EXPERTS - 1))

    def part(ref, at, h):
        return ref.at[at, pl.ds(pl.multiple_of(h * part_rows, part_rows), part_rows), :]

    def ring_copy(way, step, h, source):
        to = (z + (1 if way == 0 else Z_DIM - 1)) % Z_DIM
        return pltpu.make_async_remote_copy(
            src_ref=part(column, source, h),
            dst_ref=part(column, source, h),
            send_sem=ring_send.at[way, step, h],
            recv_sem=ring_recv.at[way, step, h],
            device_id=(dp, to * X_DIM + x),
            device_id_type=MESH,
        )

    def ring_source(way, step):
        return (z + (Z_DIM - step if way == 0 else step)) % Z_DIM

    def serve_copy(source, h, sender, target):
        return pltpu.make_async_remote_copy(
            src_ref=part(column, source, h),
            dst_ref=part(served, sender, h),
            send_sem=serve_send.at[source, h],
            recv_sem=serve_recv.at[sender, h],
            device_id=(target, own),
            device_id_type=MESH,
        )

    def serve_own(h):
        return pltpu.make_async_copy(part(column, dp, h), part(served, dp, h), serve_local.at[h])

    def serve(source, h):
        @pl.when(source != dp)
        def _():
            serve_copy(source, h, dp, source).start()

        @pl.when(source == dp)
        def _():
            serve_own(h).start()

    def ring_start(h):
        for way in (0, 1):
            ring_copy(way, 0, h, z).start()
        serve(z, h)

    def ring_hop(step, h, parity):
        for way in (0, 1):
            if step == 3 and way != parity:
                continue
            source = ring_source(way, step + 1)
            ring_copy(way, step, h, source).wait_recv()
            if step < 2 or (step == 2 and way == parity):
                ring_copy(way, step + 1, h, source).start()
            serve(source, h)

    def ring_waves(first, last):
        @pl.loop(first, last)
        def _(v):
            for step in range(3):
                for parity in (0, 1):
                    ring_hop(step, 2 * v + parity, parity)

            @pl.when(v < WAVES // 2 - 1)
            def _():
                for parity in (0, 1):
                    ring_start(2 * v + 2 + parity)

            for parity in (0, 1):
                ring_hop(3, 2 * v + parity, parity)

    for parity in (0, 1):
        ring_start(parity)

    tok_count = tokens_ref.shape[0]

    def tok_copy(n):
        return pltpu.make_async_remote_copy(
            src_ref=outgoing.at[slot_rows(n), :],
            dst_ref=slots.at[slot_rows(mirror(n)), :],
            send_sem=tok_send.at[n],
            recv_sem=tok_recv.at[mirror(n)],
            device_id=plane_peer(place(n)),
            device_id_type=MESH,
        )

    named = named_ref[...]
    ids = lax.broadcasted_iota(jnp.int32, (EXPERTS, tok_count), 0)
    hits = [ids == named[k : k + 1, :] for k in (0, 1)]
    both = jnp.where(hits[0] | hits[1], 1.0, 0.0).astype(jnp.bfloat16)
    row = lax.broadcasted_iota(jnp.int32, (tok_count, tok_count), 0)
    col = lax.broadcasted_iota(jnp.int32, (tok_count, tok_count), 1)
    earlier = jnp.where(row < col, 1.0, 0.0).astype(jnp.bfloat16)
    before = jnp.dot(both, earlier, preferred_element_type=jnp.float32)
    wide = [
        named[k : k + 1, :].astype(jnp.float32) * cap
        + jnp.sum(jnp.where(hits[k], before, 0.0), axis=0, keepdims=True)
        for k in (0, 1)
    ]
    loads[4].wait()
    group = 8 * cap
    width = tokens_ref.shape[1]
    chunk = 1024

    @pl.loop(0, 4)
    def _(q):
        row_id = q * group + lax.broadcasted_iota(jnp.int32, (group, tok_count), 0)
        slot_id = slot_ids(row_id)
        pick = jnp.where((slot_id == wide[0]) | (slot_id == wide[1]), 1.0, 0.0).astype(jnp.bfloat16)
        for c in range(width // chunk):
            outgoing[pl.ds(pl.multiple_of(q * group, group), group), c * chunk : (c + 1) * chunk] = (
                jnp.dot(
                    pick,
                    tokens_ref[:, c * chunk : (c + 1) * chunk],
                    preferred_element_type=jnp.float32,
                ).astype(jnp.bfloat16)
            )

        @pl.loop(0, 8)
        def _(i):
            n = q * 8 + i

            @pl.when(n > 0)
            def _():
                tok_copy(n).start()

    slots[slot_rows(0), :] = outgoing[slot_rows(0), :]

    def one_copy(j, sender):
        return pltpu.make_async_remote_copy(
            src_ref=spread.at[j],
            dst_ref=landed.at[sender],
            send_sem=one_send.at[j],
            recv_sem=one_recv.at[sender],
            device_id=(dp, j),
            device_id_type=MESH,
        )

    def two_copy(j, sender):
        return pltpu.make_async_remote_copy(
            src_ref=chosen.at[j],
            dst_ref=final_ref.at[sender],
            send_sem=two_send.at[j],
            recv_sem=two_recv.at[sender],
            device_id=(dp, j),
            device_id_type=MESH,
        )

    two_own = pltpu.make_async_copy(chosen.at[own], final_ref.at[own], two_local)

    ring_waves(0, 1)

    @pl.loop(1, EXPERTS)
    def _(o):
        one_copy(owner(o), own).start()

    ring_waves(1, WAVES // 2)

    @pl.loop(1, EXPERTS)
    def _(o):
        p = (own + EXPERTS - o) % EXPERTS
        one_copy(p, p).wait_recv()

    @pl.loop(0, EXPERTS)
    def _(j):
        chosen[j] = landed[placement_ref[j]]

    @pl.loop(1, EXPERTS)
    def _(o):
        two_copy(owner(o), own).start()

    two_own.start()

    def served_parts(first, last):
        @pl.loop(0, DP)
        def _(s):
            @pl.when(s != dp)
            def _():
                @pl.loop(first, last)
                def _(h):
                    serve_copy(dp, h, s, s).wait_recv()

            @pl.when(s == dp)
            def _():
                @pl.loop(first, last)
                def _(h):
                    serve_own(h).wait()

    def product(rows, n, depths):
        right = jnp.concatenate([served[2 * n, depths, :], served[2 * n + 1, depths, :]], axis=1)
        return jnp.dot(slots[rows, depths], right, preferred_element_type=jnp.float32)

    early = WAVES - LATE
    first_depths = slice(0, early * part_rows)
    last_depths = slice(early * part_rows, width)
    served_parts(0, early)

    @pl.loop(0, 4)
    def _(q):
        base = q * 8
        rows = pl.ds(pl.multiple_of(q * group, group), group)

        @pl.loop(0, 8)
        def _(i):
            n = base + i

            @pl.when(n > 0)
            def _():
                tok_copy(mirror(n)).wait_recv()

        @pl.loop(0, DP // 2)
        def _(n):
            total[rows, pl.ds(pl.multiple_of(n * 256, 256), 256)] = product(rows, n, first_depths)

    served_parts(early, WAVES)

    def ret_copy(n):
        return pltpu.make_async_remote_copy(
            src_ref=acts.at[slot_rows(n), :],
            dst_ref=back.at[slot_rows(mirror(n)), :],
            send_sem=ret_send.at[n],
            recv_sem=ret_recv.at[mirror(n)],
            device_id=plane_peer(place(n)),
            device_id_type=MESH,
        )

    @pl.loop(0, 4)
    def _(q):
        base = q * 8
        rows = pl.ds(pl.multiple_of(q * group, group), group)

        @pl.loop(0, DP // 2)
        def _(n):
            cols = pl.ds(pl.multiple_of(n * 256, 256), 256)
            value = total[rows, cols] + product(rows, n, last_depths)
            acts[rows, cols] = (value / (1.0 + jnp.exp(-value))).astype(jnp.bfloat16)

        @pl.loop(0, 8)
        def _(i):
            n = base + i

            @pl.when(n > 0)
            def _():
                ret_copy(n).start()

    back[slot_rows(0), :] = acts[slot_rows(0), :]

    gains = gains_ref[...]
    flat = jnp.concatenate(
        [wide[0], wide[1], gains, jnp.zeros((4, tok_count), jnp.float32)], axis=0
    )
    tall = flat.T
    sums = pl.ds(0, tok_count)
    total[sums, :] = jnp.zeros((tok_count, total.shape[1]), jnp.float32)
    lane = lax.broadcasted_iota(jnp.int32, (tok_count, group), 1)

    @pl.loop(0, 4)
    def _(q):
        @pl.loop(0, 8)
        def _(i):
            n = q * 8 + i

            @pl.when(n > 0)
            def _():
                ret_copy(mirror(n)).wait_recv()

        rows = pl.ds(pl.multiple_of(q * group, group), group)
        slot_id = slot_ids(q * group + lane)
        for c in range(2):
            cols = slice(c * 512, (c + 1) * 512)
            got = [
                jnp.dot(
                    jnp.where(slot_id == tall[:, k : k + 1], 1.0, 0.0).astype(jnp.bfloat16),
                    back[rows, cols],
                    preferred_element_type=jnp.float32,
                )
                for k in (0, 1)
            ]
            total[sums, cols] += tall[:, 2:3] * got[0] + tall[:, 3:4] * got[1]

    mixed_ref[...] = total[sums, :].astype(jnp.bfloat16)

    @pl.loop(1, EXPERTS)
    def _(o):
        tok_copy(o).wait_send()
        ret_copy(o).wait_send()
        j = (own + o) % EXPERTS
        one_copy(j, own).wait_send()
        two_copy(j, own).wait_send()

    @pl.loop(0, WAVES // 2)
    def _(v):
        for parity in (0, 1):
            for step in range(4):
                for way in (0, 1):
                    if step < 3 or way == parity:
                        ring_copy(way, step, 2 * v + parity, ring_source(way, step)).wait_send()

    @pl.loop(0, Z_DIM)
    def _(s):
        @pl.when(s != dp)
        def _():
            @pl.loop(0, WAVES)
            def _(h):
                serve_copy(s, h, dp, s).wait_send()

    @pl.loop(1, EXPERTS)
    def _(o):
        p = (own + EXPERTS - o) % EXPERTS
        two_copy(p, p).wait_recv()

    two_own.wait()


def shards(
    tokens, routes, route_weights, placement, expert_weights, grads, first_moment, second_moment
):
    depth, piece = expert_weights.shape[1:]
    count, width = tokens.shape
    hidden = DP * piece
    cap = 4 * count // EXPERTS
    block = depth // EXPERTS
    vmem = pl.BlockSpec(memory_space=pltpu.VMEM)
    hbm = pl.BlockSpec(memory_space=pl.ANY)
    dma = pltpu.SemaphoreType.DMA
    mixed, final = pl.pallas_call(
        kernel,
        out_shape=(
            jax.ShapeDtypeStruct((count, hidden), jnp.bfloat16),
            jax.ShapeDtypeStruct((EXPERTS, 3 * block, piece), jnp.bfloat16),
        ),
        in_specs=[pl.BlockSpec(memory_space=pltpu.SMEM)] + [vmem] * 2 + [hbm] * 5,
        out_specs=(vmem, hbm),
        scratch_shapes=[
            pltpu.VMEM((count, width), jnp.bfloat16),
        ]
        + [pltpu.VMEM((depth, piece), jnp.bfloat16)] * 4
        + [
            pltpu.VMEM((EXPERTS * cap, hidden), jnp.float32),
            pltpu.VMEM((Z_DIM, depth, piece), jnp.bfloat16),
            pltpu.VMEM((DP, depth, piece), jnp.bfloat16),
            pltpu.VMEM((EXPERTS * cap, width), jnp.bfloat16),
            pltpu.VMEM((EXPERTS * cap, width), jnp.bfloat16),
            pltpu.VMEM((EXPERTS * cap, hidden), jnp.bfloat16),
            pltpu.VMEM((EXPERTS * cap, hidden), jnp.bfloat16),
            pltpu.VMEM((EXPERTS, 3 * block, piece), jnp.bfloat16),
            pltpu.VMEM((EXPERTS, 3 * block, piece), jnp.bfloat16),
            pltpu.VMEM((EXPERTS, 3 * block, piece), jnp.bfloat16),
            dma((2, 4, WAVES)),
            dma((2, 4, WAVES)),
            dma((Z_DIM, WAVES)),
            dma((DP, WAVES)),
            dma((WAVES,)),
        ]
        + [dma((EXPERTS,))] * 8
        + [dma, dma((5,))],
        compiler_params=pltpu.CompilerParams(
            collective_id=0, has_side_effects=True, vmem_limit_bytes=60 * 1024 * 1024
        ),
    )(
        placement, routes.T, route_weights.T, tokens,
        expert_weights[0], grads[0], first_moment[0], second_moment[0],
    )
    state = final.reshape(EXPERTS, 3, block, piece)
    return tuple(state[:, i].reshape(1, depth, piece) for i in range(3)) + (mixed,)


def solution(mesh):
    rows = P(("dp", "expert"), None)
    state = P("expert", None, "dp")
    return jax.shard_map(
        shards,
        mesh=mesh,
        in_specs=(rows, rows, rows, P(), state, state, state, state),
        out_specs=(state, state, state, rows),
        check_vma=False,
    )
```

```python
import jax
import jax.numpy as jnp
from jax import lax
from jax.experimental import pallas as pl
from jax.experimental.pallas import tpu as pltpu
from jax.sharding import PartitionSpec as P

beta_one = 0.9
beta_two = 0.999
learn_rate = 0.008
adam_eps = 1e-08

DP = 8
Z_DIM = 8
X_DIM = 4
EXPERTS = Z_DIM * X_DIM
WAVES = 4
LATE = 1
MESH = pl.DeviceIdType.MESH


def kernel(
    placement_ref, named_ref, gains_ref, tokens_in, w_in, g_in, m_in, v_in,
    mixed_ref, final_ref,
    tokens_ref, w_ref, g_ref, m_ref, v_ref, total,
    column, served, outgoing, slots, acts, back, spread, landed, chosen,
    ring_send, ring_recv, serve_send, serve_recv, serve_local,
    tok_send, tok_recv, ret_send, ret_recv, one_send, one_recv, two_send, two_recv, two_local, load,
):
    dp = lax.axis_index("dp")
    own = lax.axis_index("expert")
    z, x = own // X_DIM, own % X_DIM
    mine = dp * X_DIM + x
    cap = slots.shape[0] // EXPERTS
    block = spread.shape[1] // 3
    part_rows = column.shape[1] // WAVES

    def plane_peer(p):
        return (p // X_DIM, z * X_DIM + p % X_DIM)

    def slot_rows(p):
        return pl.ds(pl.multiple_of(p * cap, cap), cap)

    loads = [
        pltpu.make_async_copy(source, target, load.at[i])
        for i, (source, target) in enumerate(
            (
                (w_in, w_ref), (g_in, g_ref), (m_in, m_ref), (v_in, v_ref), (tokens_in, tokens_ref)
            )
        )
    ]
    for copy in loads:
        copy.start()

    def place(n):
        y_step, x_step = n % 4, (n // 4 + n) % 4
        chip_y, core = (dp // 2 + y_step) % 4, (dp + n // 16) % 2
        return (chip_y * 2 + core) * X_DIM + (x + x_step) % X_DIM

    def mirror(n):
        y_step, x_step = (4 - n % 4) % 4, (8 - (n // 4) % 4 - n % 4) % 4
        return (n // 16) * 16 + ((x_step + 4 - y_step) % 4) * 4 + y_step

    def slot_ids(row):
        n = row >> 5
        y_step, x_step = n & 3, ((n >> 2) + n) & 3
        chip_y, core = (dp // 2 + y_step) & 3, (dp + (n >> 4)) & 1
        served_by = (chip_y * 2 + core) * X_DIM + ((x + x_step) & 3)
        return (served_by * cap + (row & (cap - 1))).astype(jnp.float32)

    def owner(n):
        k = n % Z_DIM
        z_step = (k % 2) * ((k + 1) // 2) + (1 - k % 2) * (Z_DIM - k // 2)
        return ((z + z_step) % Z_DIM) * X_DIM + (x + n // Z_DIM + n) % X_DIM

    barrier = pltpu.get_barrier_semaphore()

    @pl.loop(1, EXPERTS)
    def _(o):
        pl.semaphore_signal(
            barrier, inc=1, device_id=plane_peer((mine + o) % EXPERTS), device_id_type=MESH
        )
        pl.semaphore_signal(
            barrier, inc=1, device_id=(dp, (own + o) % EXPERTS), device_id_type=MESH
        )

    pl.semaphore_wait(barrier, 2 * (EXPERTS - 1))

    def part(ref, at, h):
        return ref.at[at, pl.ds(pl.multiple_of(h * part_rows, part_rows), part_rows), :]

    def ring_copy(way, step, h, source):
        to = (z + (1 if way == 0 else Z_DIM - 1)) % Z_DIM
        return pltpu.make_async_remote_copy(
            src_ref=part(column, source, h),
            dst_ref=part(column, source, h),
            send_sem=ring_send.at[way, step, h],
            recv_sem=ring_recv.at[way, step, h],
            device_id=(dp, to * X_DIM + x),
            device_id_type=MESH,
        )

    def ring_source(way, step):
        return (z + (Z_DIM - step if way == 0 else step)) % Z_DIM

    def serve_copy(source, h, sender, target):
        return pltpu.make_async_remote_copy(
            src_ref=part(column, source, h),
            dst_ref=part(served, sender, h),
            send_sem=serve_send.at[source, h],
            recv_sem=serve_recv.at[sender, h],
            device_id=(target, own),
            device_id_type=MESH,
        )

    def serve_own(h):
        return pltpu.make_async_copy(part(column, dp, h), part(served, dp, h), serve_local.at[h])

    def serve(source, h):
        @pl.when(source != dp)
        def _():
            serve_copy(source, h, dp, source).start()

        @pl.when(source == dp)
        def _():
            serve_own(h).start()

    def ring_start(h):
        for way in (0, 1):
            ring_copy(way, 0, h, z).start()
        serve(z, h)

    def ring_hop(step, h, parity):
        for way in (0, 1):
            if step == 3 and way != parity:
                continue
            source = ring_source(way, step + 1)
            ring_copy(way, step, h, source).wait_recv()
            if step < 2 or (step == 2 and way == parity):
                ring_copy(way, step + 1, h, source).start()
            serve(source, h)

    def ring_waves(first, last):
        @pl.loop(first, last)
        def _(v):
            for step in range(3):
                for parity in (0, 1):
                    ring_hop(step, 2 * v + parity, parity)

            @pl.when(v < WAVES // 2 - 1)
            def _():
                for parity in (0, 1):
                    ring_start(2 * v + 2 + parity)

            for parity in (0, 1):
                ring_hop(3, 2 * v + parity, parity)

    tok_count = tokens_ref.shape[0]

    def tok_copy(n):
        return pltpu.make_async_remote_copy(
            src_ref=outgoing.at[slot_rows(n), :],
            dst_ref=slots.at[slot_rows(mirror(n)), :],
            send_sem=tok_send.at[n],
            recv_sem=tok_recv.at[mirror(n)],
            device_id=plane_peer(place(n)),
            device_id_type=MESH,
        )

    named = named_ref[...]
    ids = lax.broadcasted_iota(jnp.int32, (EXPERTS, tok_count), 0)
    hits = [ids == named[k : k + 1, :] for k in (0, 1)]
    both = jnp.where(hits[0] | hits[1], 1.0, 0.0).astype(jnp.bfloat16)
    row = lax.broadcasted_iota(jnp.int32, (tok_count, tok_count), 0)
    col = lax.broadcasted_iota(jnp.int32, (tok_count, tok_count), 1)
    earlier = jnp.where(row < col, 1.0, 0.0).astype(jnp.bfloat16)
    before = jnp.dot(both, earlier, preferred_element_type=jnp.float32)
    wide = [
        named[k : k + 1, :].astype(jnp.float32) * cap
        + jnp.sum(jnp.where(hits[k], before, 0.0), axis=0, keepdims=True)
        for k in (0, 1)
    ]
    loads[4].wait()
    group = 8 * cap
    width = tokens_ref.shape[1]
    chunk = 1024

    @pl.loop(0, 4)
    def _(q):
        row_id = q * group + lax.broadcasted_iota(jnp.int32, (group, tok_count), 0)
        slot_id = slot_ids(row_id)
        pick = jnp.where((slot_id == wide[0]) | (slot_id == wide[1]), 1.0, 0.0).astype(jnp.bfloat16)
        for c in range(width // chunk):
            outgoing[pl.ds(pl.multiple_of(q * group, group), group), c * chunk : (c + 1) * chunk] = (
                jnp.dot(
                    pick,
                    tokens_ref[:, c * chunk : (c + 1) * chunk],
                    preferred_element_type=jnp.float32,
                ).astype(jnp.bfloat16)
            )

        @pl.loop(0, 8)
        def _(i):
            n = q * 8 + i

            @pl.when(n > 0)
            def _():
                tok_copy(n).start()

    slots[slot_rows(0), :] = outgoing[slot_rows(0), :]

    for copy in loads[:4]:
        copy.wait()

    @pl.loop(0, EXPERTS)
    def _(j):
        rows = pl.ds(pl.multiple_of(j * block, block), block)
        grad = g_ref[rows, :].astype(jnp.float32)
        first = beta_one * m_ref[rows, :].astype(jnp.float32) + (1.0 - beta_one) * grad
        second = beta_two * v_ref[rows, :].astype(jnp.float32) + (1.0 - beta_two) * grad * grad
        updated = w_ref[rows, :].astype(jnp.float32) - learn_rate * first / (
            jnp.sqrt(second) + adam_eps
        )
        updated = updated.astype(jnp.bfloat16)
        column[z, rows, :] = updated
        spread[j, 0:block, :] = updated
        spread[j, block : 2 * block, :] = first.astype(jnp.bfloat16)
        spread[j, 2 * block : 3 * block, :] = second.astype(jnp.bfloat16)

    landed[own] = spread[own]
    for parity in (0, 1):
        ring_start(parity)

    def one_copy(j, sender):
        return pltpu.make_async_remote_copy(
            src_ref=spread.at[j],
            dst_ref=landed.at[sender],
            send_sem=one_send.at[j],
            recv_sem=one_recv.at[sender],
            device_id=(dp, j),
            device_id_type=MESH,
        )

    def two_copy(j, sender):
        return pltpu.make_async_remote_copy(
            src_ref=chosen.at[j],
            dst_ref=final_ref.at[sender],
            send_sem=two_send.at[j],
            recv_sem=two_recv.at[sender],
            device_id=(dp, j),
            device_id_type=MESH,
        )

    two_own = pltpu.make_async_copy(chosen.at[own], final_ref.at[own], two_local)

    ring_waves(0, 1)

    @pl.loop(1, EXPERTS)
    def _(o):
        one_copy(owner(o), own).start()

    ring_waves(1, WAVES // 2)

    @pl.loop(1, EXPERTS)
    def _(o):
        p = (own + EXPERTS - o) % EXPERTS
        one_copy(p, p).wait_recv()

    @pl.loop(0, EXPERTS)
    def _(j):
        chosen[j] = landed[placement_ref[j]]

    @pl.loop(1, EXPERTS)
    def _(o):
        two_copy(owner(o), own).start()

    two_own.start()

    def served_parts(first, last):
        @pl.loop(0, DP)
        def _(s):
            @pl.when(s != dp)
            def _():
                @pl.loop(first, last)
                def _(h):
                    serve_copy(dp, h, s, s).wait_recv()

            @pl.when(s == dp)
            def _():
                @pl.loop(first, last)
                def _(h):
                    serve_own(h).wait()

    def product(rows, n, depths):
        right = jnp.concatenate([served[2 * n, depths, :], served[2 * n + 1, depths, :]], axis=1)
        return jnp.dot(slots[rows, depths], right, preferred_element_type=jnp.float32)

    early = WAVES - LATE
    first_depths = slice(0, early * part_rows)
    last_depths = slice(early * part_rows, width)
    served_parts(0, early)

    @pl.loop(0, 4)
    def _(q):
        base = q * 8
        rows = pl.ds(pl.multiple_of(q * group, group), group)

        @pl.loop(0, 8)
        def _(i):
            n = base + i

            @pl.when(n > 0)
            def _():
                tok_copy(mirror(n)).wait_recv()

        @pl.loop(0, DP // 2)
        def _(n):
            total[rows, pl.ds(pl.multiple_of(n * 256, 256), 256)] = product(rows, n, first_depths)

    served_parts(early, WAVES)

    def ret_copy(n):
        return pltpu.make_async_remote_copy(
            src_ref=acts.at[slot_rows(n), :],
            dst_ref=back.at[slot_rows(mirror(n)), :],
            send_sem=ret_send.at[n],
            recv_sem=ret_recv.at[mirror(n)],
            device_id=plane_peer(place(n)),
            device_id_type=MESH,
        )

    @pl.loop(0, 4)
    def _(q):
        base = q * 8
        rows = pl.ds(pl.multiple_of(q * group, group), group)

        @pl.loop(0, DP // 2)
        def _(n):
            cols = pl.ds(pl.multiple_of(n * 256, 256), 256)
            value = total[rows, cols] + product(rows, n, last_depths)
            acts[rows, cols] = (value / (1.0 + jnp.exp(-value))).astype(jnp.bfloat16)

        @pl.loop(0, 8)
        def _(i):
            n = base + i

            @pl.when(n > 0)
            def _():
                ret_copy(n).start()

    back[slot_rows(0), :] = acts[slot_rows(0), :]

    gains = gains_ref[...]
    flat = jnp.concatenate(
        [wide[0], wide[1], gains, jnp.zeros((4, tok_count), jnp.float32)], axis=0
    )
    tall = flat.T
    sums = pl.ds(0, tok_count)
    total[sums, :] = jnp.zeros((tok_count, total.shape[1]), jnp.float32)
    lane = lax.broadcasted_iota(jnp.int32, (tok_count, group), 1)

    @pl.loop(0, 4)
    def _(q):
        @pl.loop(0, 8)
        def _(i):
            n = q * 8 + i

            @pl.when(n > 0)
            def _():
                ret_copy(mirror(n)).wait_recv()

        rows = pl.ds(pl.multiple_of(q * group, group), group)
        slot_id = slot_ids(q * group + lane)
        for c in range(2):
            cols = slice(c * 512, (c + 1) * 512)
            got = [
                jnp.dot(
                    jnp.where(slot_id == tall[:, k : k + 1], 1.0, 0.0).astype(jnp.bfloat16),
                    back[rows, cols],
                    preferred_element_type=jnp.float32,
                )
                for k in (0, 1)
            ]
            total[sums, cols] += tall[:, 2:3] * got[0] + tall[:, 3:4] * got[1]

    mixed_ref[...] = total[sums, :].astype(jnp.bfloat16)

    @pl.loop(1, EXPERTS)
    def _(o):
        tok_copy(o).wait_send()
        ret_copy(o).wait_send()
        j = (own + o) % EXPERTS
        one_copy(j, own).wait_send()
        two_copy(j, own).wait_send()

    @pl.loop(0, WAVES // 2)
    def _(v):
        for parity in (0, 1):
            for step in range(4):
                for way in (0, 1):
                    if step < 3 or way == parity:
                        ring_copy(way, step, 2 * v + parity, ring_source(way, step)).wait_send()

    @pl.loop(0, Z_DIM)
    def _(s):
        @pl.when(s != dp)
        def _():
            @pl.loop(0, WAVES)
            def _(h):
                serve_copy(s, h, dp, s).wait_send()

    @pl.loop(1, EXPERTS)
    def _(o):
        p = (own + EXPERTS - o) % EXPERTS
        two_copy(p, p).wait_recv()

    two_own.wait()


def shards(
    tokens, routes, route_weights, placement, expert_weights, grads, first_moment, second_moment
):
    depth, piece = expert_weights.shape[1:]
    count, width = tokens.shape
    hidden = DP * piece
    cap = 4 * count // EXPERTS
    block = depth // EXPERTS
    vmem = pl.BlockSpec(memory_space=pltpu.VMEM)
    hbm = pl.BlockSpec(memory_space=pl.ANY)
    dma = pltpu.SemaphoreType.DMA
    mixed, final = pl.pallas_call(
        kernel,
        out_shape=(
            jax.ShapeDtypeStruct((count, hidden), jnp.bfloat16),
            jax.ShapeDtypeStruct((EXPERTS, 3 * block, piece), jnp.bfloat16),
        ),
        in_specs=[pl.BlockSpec(memory_space=pltpu.SMEM)] + [vmem] * 2 + [hbm] * 5,
        out_specs=(vmem, hbm),
        scratch_shapes=[
            pltpu.VMEM((count, width), jnp.bfloat16),
        ]
        + [pltpu.VMEM((depth, piece), jnp.bfloat16)] * 4
        + [
            pltpu.VMEM((EXPERTS * cap, hidden), jnp.float32),
            pltpu.VMEM((Z_DIM, depth, piece), jnp.bfloat16),
            pltpu.VMEM((DP, depth, piece), jnp.bfloat16),
            pltpu.VMEM((EXPERTS * cap, width), jnp.bfloat16),
            pltpu.VMEM((EXPERTS * cap, width), jnp.bfloat16),
            pltpu.VMEM((EXPERTS * cap, hidden), jnp.bfloat16),
            pltpu.VMEM((EXPERTS * cap, hidden), jnp.bfloat16),
            pltpu.VMEM((EXPERTS, 3 * block, piece), jnp.bfloat16),
            pltpu.VMEM((EXPERTS, 3 * block, piece), jnp.bfloat16),
            pltpu.VMEM((EXPERTS, 3 * block, piece), jnp.bfloat16),
            dma((2, 4, WAVES)),
            dma((2, 4, WAVES)),
            dma((Z_DIM, WAVES)),
            dma((DP, WAVES)),
            dma((WAVES,)),
        ]
        + [dma((EXPERTS,))] * 8
        + [dma, dma((5,))],
        compiler_params=pltpu.CompilerParams(
            collective_id=0, has_side_effects=True, vmem_limit_bytes=60 * 1024 * 1024
        ),
    )(
        placement, routes.T, route_weights.T, tokens,
        expert_weights[0], grads[0], first_moment[0], second_moment[0],
    )
    state = final.reshape(EXPERTS, 3, block, piece)
    return tuple(state[:, i].reshape(1, depth, piece) for i in range(3)) + (mixed,)


def solution(mesh):
    rows = P(("dp", "expert"), None)
    state = P("expert", None, "dp")
    return jax.shard_map(
        shards,
        mesh=mesh,
        in_specs=(rows, rows, rows, P(), state, state, state, state),
        out_specs=(state, state, state, rows),
        check_vma=False,
    )
```
